32 devices in a mesh: dp: 8 (over y, x, core), group: 4 (over z).
Axes of the slice: x: 2, y: 2, z: 4, core: 2. Of those that a mesh axis runs over, the one named last changes fastest.
Arguments:
- patches: bfloat16 [53248, 768], P('dp', 'group'), may hold values from -4 to 4
- embed_weight: bfloat16 [768, 1024], P('dp', 'group'), may hold values from -0.0625 to 0.0625
- channel_gain: float32 [1024], replicated, may hold values from 0.1 to 1.9
- cotangent: bfloat16 [53248, 1024], P('dp', 'group'), may hold values from -6 to 6
Outputs:
- weight_grad: float32 [768, 1024], P('dp', 'group')
- gain_grad: float32 [1024], P('group')
The draws below stay inside these ranges and needn't reach their ends.
All inputs are finite; a program needn't handle non-finite values.
Results may differ from the reference program's by a relative error of at most 0.00155.
Values may be sent and summed in bfloat16 or wider, within the bound.
A program may use at most 128 MiB of HBM per device.

```python
import math
import jax
import jax.numpy as jnp
from jax import lax

PD = 768
G = 16
GW = 64
ITERS = 5
C = 1024
TOKENS = 53248


def patch_noise(key):
    sub = jax.random.fold_in(key, 101)
    return jnp.clip(jax.random.normal(sub, (TOKENS, PD), jnp.float32), -3.0, 3.0)


def patch_offset(key):
    sub = jax.random.fold_in(key, 102)
    return jax.random.uniform(sub, (PD,), jnp.float32, -1.0, 1.0)


def weight_values(key):
    sub = jax.random.fold_in(key, 103)
    bound = 0.99 * jnp.sqrt(3.0 / PD)
    return jax.random.uniform(sub, (PD, G * GW), jnp.float32, -bound, bound)


def draw_patches(key, part):
    return (patch_noise(key) + patch_offset(key)[None, :]).astype(jnp.bfloat16)


def draw_embed_weight(key, part):
    return weight_values(key).astype(jnp.bfloat16)


def draw_cotangent(key, part):
    weights = weight_values(key)
    features = jnp.dot(patch_noise(key), weights)
    features = features / jnp.sqrt(jnp.sum(weights * weights, axis=0))
    mixing = jax.random.normal(jax.random.fold_in(key, 104), (G, GW, GW), jnp.float32)
    mixing = mixing * (1.0 - jnp.eye(GW, dtype=jnp.float32)) / jnp.sqrt(GW - 1.0)
    related = jnp.einsum('tgb,gab->tga', features.reshape(TOKENS, G, GW), mixing).reshape(TOKENS, G * GW)
    noise_key = jax.random.fold_in(key, 105)
    offset_key = jax.random.fold_in(key, 106)
    noise = jnp.clip(jax.random.normal(noise_key, (TOKENS, G * GW), jnp.float32), -3.5, 3.5)
    offset = jax.random.uniform(offset_key, (G * GW,), jnp.float32, -0.7, 0.7)
    return jnp.clip(noise + offset[None, :] + 0.3 * related, -6.0, 6.0).astype(jnp.bfloat16)


def setup_inputs(seed: int = 0) -> dict:
    keys = jax.random.split(jax.random.key(seed), 5)
    return {
        "patches": draw_patches(jax.random.fold_in(keys[4], 71), 0),
        "embed_weight": draw_embed_weight(jax.random.fold_in(keys[4], 71), 0),
        "channel_gain": jnp.clip(1.0 + 0.18 * jax.random.normal(keys[2], (C,), jnp.float32), 0.1, 1.9),
        "cotangent": draw_cotangent(jax.random.fold_in(keys[4], 71), 0),
    }


EPSILON = 1e-05
highest = lax.Precision.HIGHEST

def matmul_batch(left, right):
    return jnp.einsum('gij,gjk->gik', left, right, precision=highest)

def whiten_matrix(covariance):
    width = covariance.shape[-1]
    traces = jnp.trace(covariance, axis1=1, axis2=2)
    normed = covariance / traces[:, None, None]
    iterate = jnp.broadcast_to(jnp.eye(width, dtype=jnp.float32), covariance.shape)
    for counter in range(ITERS):
        cubed = matmul_batch(matmul_batch(iterate, iterate), iterate)
        iterate = 1.5 * iterate - 0.5 * matmul_batch(cubed, normed)
    return iterate / jnp.sqrt(traces)[:, None, None]

def forward(features, channel_gain):
    tok_rows = features.shape[0]
    average = lax.optimization_barrier(jnp.sum(features, axis=0)) / TOKENS
    centered = features - average
    grouped = centered.reshape(tok_rows, G, GW)
    covariance = jnp.einsum('tga,tgb->gab', grouped, grouped, precision=highest) / TOKENS
    covariance = covariance + EPSILON * jnp.eye(GW, dtype=jnp.float32)
    whitener = whiten_matrix(covariance)
    whitened = jnp.einsum('tgb,gab->tga', grouped, whitener, precision=highest)
    return whitened.reshape(tok_rows, G * GW) * channel_gain

def reference(patches, embed_weight, channel_gain, cotangent):
    embedded = jnp.dot(patches, embed_weight, preferred_element_type=jnp.float32).astype(jnp.bfloat16)
    outputs, pullback = jax.vjp(forward, embedded.astype(jnp.float32), channel_gain)
    grad_out = cotangent.astype(jnp.float32) * (1.0 / math.sqrt(TOKENS))
    grad_feat, gain_grad = pullback(grad_out)
    weight_grad = jnp.dot(patches.T, grad_feat.astype(jnp.bfloat16), preferred_element_type=jnp.float32)
    return (weight_grad, gain_grad)
```

```python
import math

import jax
import jax.numpy as jnp
from jax import lax
from jax.sharding import PartitionSpec as P

GW = 64
ITERS = 5


EPSILON = 1e-05
highest = lax.Precision.HIGHEST


def matmul_batch(left, right):
    return jnp.einsum("gij,gjk->gik", left, right, precision=highest)


def whiten_matrix(covariance):
    width = covariance.shape[-1]
    traces = jnp.trace(covariance, axis1=1, axis2=2)
    normed = covariance / traces[:, None, None]
    iterate = jnp.broadcast_to(jnp.eye(width, dtype=jnp.float32), covariance.shape)
    for counter in range(ITERS):
        cubed = matmul_batch(matmul_batch(iterate, iterate), iterate)
        iterate = 1.5 * iterate - 0.5 * matmul_batch(cubed, normed)
    return iterate / jnp.sqrt(traces)[:, None, None]


def block_diagonals(square):
    width = square.shape[0]
    groups = width // GW
    blocks = square.reshape(groups, GW, groups, GW)
    return jnp.stack([blocks[g, :, g, :] for g in range(groups)])


def contract_tokens(left, right):
    return lax.dot_general(
        left, right, (((0,), (0,)), ((), ())), preferred_element_type=jnp.float32
    )


def body(patches, embed_weight, channel_gain, cotangent):
    tok_rows = patches.shape[0]
    total_tokens = tok_rows * lax.axis_size("dp")
    loss_scale = 1.0 / math.sqrt(total_tokens)
    identity = jnp.eye(GW, dtype=jnp.float32)
    width_here = embed_weight.shape[1]
    weights = lax.all_gather(embed_weight, "dp", axis=0, tiled=True)
    full_patches = lax.all_gather(patches, "group", axis=1, tiled=True)
    gain_here = lax.dynamic_slice_in_dim(
        channel_gain, lax.axis_index("group") * width_here, width_here
    )
    embedded = jnp.dot(full_patches, weights, preferred_element_type=jnp.float32).astype(
        jnp.bfloat16
    )
    both = jnp.concatenate([embedded, cotangent], axis=1)
    stats = contract_tokens(embedded, both)
    raw_products = block_diagonals(stats[:, :width_here])
    cross = jnp.swapaxes(block_diagonals(stats[:, width_here:]), 1, 2)
    sums = jnp.sum(both.astype(jnp.float32), axis=0)
    raw_products, cross, sums = lax.psum((raw_products, cross, sums), "dp")
    patch_products = jnp.concatenate(
        [
            contract_tokens(full_patches, both),
            jnp.broadcast_to(
                jnp.sum(full_patches.astype(jnp.float32), axis=0)[:, None],
                (full_patches.shape[1], 128),
            ),
        ],
        axis=1,
    )
    patch_products = lax.psum_scatter(patch_products, "dp", scatter_dimension=0, tiled=True)
    return finish(
        raw_products, cross, sums, patch_products, gain_here, loss_scale, total_tokens, identity
    )


def finish(raw_products, cross, sums, patch_products, gain_here, loss_scale, total_tokens, identity):
    width_here = gain_here.shape[0]
    mean_groups = (sums[:width_here] / total_tokens).reshape(-1, GW)
    cot_sums = sums[width_here:].reshape(-1, GW)
    covariance = (
        raw_products / total_tokens
        - jnp.einsum("ga,gb->gab", mean_groups, mean_groups, precision=highest)
        + EPSILON * identity
    )
    whitener, pullback = jax.vjp(whiten_matrix, covariance)
    cross = loss_scale * (
        cross - jnp.einsum("ga,gb->gab", cot_sums, mean_groups, precision=highest)
    )
    gain_grad = jnp.sum(cross * whitener, axis=2).reshape(-1)
    scale = loss_scale * gain_here
    (grad_cov,) = pullback(cross * gain_here.reshape(-1, GW)[:, :, None])
    symmetric = (grad_cov + jnp.swapaxes(grad_cov, 1, 2)) / total_tokens
    patch_sums = patch_products[:, 2 * width_here : 2 * width_here + 1]
    rows = patch_products.shape[0]
    feat_part = patch_products[:, :width_here] - patch_sums * mean_groups.reshape(-1)
    cot_part = scale * (
        patch_products[:, width_here : 2 * width_here]
        - patch_sums * (cot_sums.reshape(-1) / total_tokens)
    )
    weight_grad = jnp.einsum(
        "rga,gab->rgb", cot_part.reshape(rows, -1, GW), whitener, precision=highest
    ) + jnp.einsum("rgb,gcb->rgc", feat_part.reshape(rows, -1, GW), symmetric, precision=highest)
    return (weight_grad.reshape(rows, -1), gain_grad)


def solution(mesh):
    placed = (P("dp", "group"), P("dp", "group"), P(), P("dp", "group"))
    return jax.shard_map(
        body, mesh=mesh, in_specs=placed, out_specs=(P("dp", "group"), P("group")), check_vma=False
    )
```

```python
import functools
import math

import jax
import jax.numpy as jnp
from jax import lax
from jax.experimental import pallas as pl
from jax.experimental.pallas import tpu as pltpu
from jax.sharding import PartitionSpec as P

GW = 64
ITERS = 5


EPSILON = 1e-05
highest = lax.Precision.HIGHEST


def matmul_batch(left, right):
    return jnp.einsum("gij,gjk->gik", left, right, precision=highest)


def whiten_matrix(covariance):
    width = covariance.shape[-1]
    traces = jnp.trace(covariance, axis1=1, axis2=2)
    normed = covariance / traces[:, None, None]
    iterate = jnp.broadcast_to(jnp.eye(width, dtype=jnp.float32), covariance.shape)
    for counter in range(ITERS):
        cubed = matmul_batch(matmul_batch(iterate, iterate), iterate)
        iterate = 1.5 * iterate - 0.5 * matmul_batch(cubed, normed)
    return iterate / jnp.sqrt(traces)[:, None, None]


def block_diagonals(square):
    width = square.shape[0]
    groups = width // GW
    blocks = square.reshape(groups, GW, groups, GW)
    return jnp.stack([blocks[g, :, g, :] for g in range(groups)])


MESH = pl.DeviceIdType.MESH
LEAD = 2


def window_of(part, depth):
    start = part * depth // 128 * 128
    stop = -(-(part + 1) * depth // 128) * 128
    return start, stop - start, part * depth - start


def token_kernel(
    n, ndp, parts, depth, chunk,
    x_hbm, cot_hbm, w_hbm,
    out_ref, stats_ref,
    held, cot, weights, padded, totals, patch_sums, bank,
    send_right, recv_right, send_left, recv_left, w_send, w_recv, local_sem,
):
    me = lax.axis_index("group")
    mine = lax.axis_index("dp")
    right, left = lax.rem(me + 1, n), lax.rem(me + n - 1, n)
    rows = x_hbm.shape[0]
    chunks = rows // chunk
    width = cot.shape[1]
    hops = n // 2
    slab = w_hbm.shape[0]

    own_x = pltpu.make_async_copy(x_hbm, held.at[0], local_sem.at[0])
    own_cot = pltpu.make_async_copy(cot_hbm, cot, local_sem.at[1])
    own_w = pltpu.make_async_copy(w_hbm, weights.at[mine], local_sem.at[2])
    own_x.start()
    own_cot.start()
    own_w.start()

    barrier = pltpu.get_barrier_semaphore()
    for step in range(1, ndp):
        pl.semaphore_signal(
            barrier, inc=1, device_id={"dp": lax.rem(mine + step, ndp)}, device_id_type=MESH
        )
    for neighbour in (left, right):
        pl.semaphore_signal(barrier, inc=1, device_id={"group": neighbour}, device_id_type=MESH)
    pl.semaphore_wait(barrier, ndp + 1)

    def w_copy(step):
        return pltpu.make_async_remote_copy(
            src_ref=w_hbm,
            dst_ref=weights.at[mine],
            send_sem=w_send.at[step],
            recv_sem=w_recv.at[step],
            device_id={"dp": lax.rem(mine + step, ndp)},
            device_id_type=MESH,
        )

    def x_copy(hop, piece, to_right):
        start, size = pl.multiple_of(piece * chunk, chunk), chunk
        if n % 2 == 0 and hop == hops:
            size = chunk // 2
            if not to_right:
                start = start + size
        span = pl.ds(pl.multiple_of(start, size), size)
        source = x_hbm.at[span] if hop == 1 else held.at[hop - 1 if to_right else n - hop + 1, span]
        send, recv = (send_right, recv_right) if to_right else (send_left, recv_left)
        return pltpu.make_async_remote_copy(
            src_ref=source,
            dst_ref=held.at[hop if to_right else n - hop, span],
            send_sem=send.at[hop - 1, piece],
            recv_sem=recv.at[hop - 1, piece],
            device_id={"group": right if to_right else left},
            device_id_type=MESH,
        )

    for step in range(1, ndp):
        w_copy(step).start()
    for piece in range(min(LEAD, chunks)):
        for to_right in (True, False):
            x_copy(1, piece, to_right).start()

    totals[...] = jnp.zeros_like(totals)
    patch_sums[...] = jnp.zeros_like(patch_sums)
    stats_ref[...] = jnp.zeros_like(stats_ref)
    padded[...] = jnp.zeros_like(padded)
    own_w.wait()
    for step in range(1, ndp):
        w_copy(step).wait()
    per = depth // slab
    for j in range(n):
        for part in range(parts):
            offset = window_of(part, depth)[2]
            for k in range(per):
                padded[j, part, offset + k * slab : offset + (k + 1) * slab, :] = weights[
                    j * per + k
                ]
    own_x.wait()
    own_cot.wait()
    ones = jnp.ones((16, chunk), jnp.bfloat16)

    def compute(piece):
        span = pl.ds(pl.multiple_of(piece * chunk, chunk), chunk)
        for part in range(parts):
            start, size, _ = window_of(part, depth)
            embedded = jnp.zeros((chunk, width), jnp.float32)
            for slot in range(n):
                origin = lax.rem(me - slot + n, n)
                embedded += jnp.dot(
                    held[slot, span, start : start + size],
                    padded[origin, part, :size, :],
                    preferred_element_type=jnp.float32,
                )
            tokens = pl.ds(pl.multiple_of(part * rows + piece * chunk, chunk), chunk)
            bank[:, :width] = embedded.astype(jnp.bfloat16)
            bank[:, width:] = cot[tokens, :]
            both = bank[...]
            flipped = both.T
            stats_ref[:width, :] += jnp.dot(
                flipped[:width], both, preferred_element_type=jnp.float32
            )
            stats_ref[width:, :] += jnp.dot(ones, both, preferred_element_type=jnp.float32)[:8]
            for slot in range(n):
                totals[slot, part, :, :size] += jnp.dot(
                    flipped,
                    held[slot, span, start : start + size],
                    preferred_element_type=jnp.float32,
                )
        for slot in range(n):
            patch_sums[slot] += jnp.dot(
                ones, held[slot, span, :], preferred_element_type=jnp.float32
            )[:8]

    def arrive(hop, piece):
        for to_right in (True, False):
            x_copy(hop, piece, to_right).wait()

    @pl.loop(0, chunks + LEAD * (hops - 1))
    def _(step):
        @pl.when(step + LEAD < chunks)
        def _():
            for to_right in (True, False):
                x_copy(1, step + LEAD, to_right).start()

        for hop in range(1, hops):
            piece = step - LEAD * (hop - 1)

            @pl.when((piece >= 0) & (piece < chunks))
            def _():
                for to_right in (True, False):
                    x_copy(hop, piece, to_right).wait_recv()
                    x_copy(hop + 1, piece, to_right).start()

        piece = step - LEAD * (hops - 1)

        @pl.when(piece >= 0)
        def _():
            for to_right in (True, False):
                x_copy(hops, piece, to_right).wait_recv()
            compute(piece)

    @pl.loop(0, chunks)
    def _(piece):
        for hop in range(1, hops + 1):
            for to_right in (True, False):
                x_copy(hop, piece, to_right).wait_send()

    for slot in range(n):
        origin = lax.rem(me - slot + n, n)
        base = pl.multiple_of(origin * depth, 8)
        gathered = None
        for part in range(parts):
            start, size, offset = window_of(part, depth)
            block = totals[slot, part, :, :size].T[offset : offset + depth]
            gathered = block if gathered is None else gathered + block
        out_ref[pl.ds(base, depth), : 2 * width] = gathered
        added = None
        for part in range(parts):
            start, size, offset = window_of(part, depth)
            line = jnp.broadcast_to(patch_sums[slot, :1, start : start + size], (128, size)).T
            line = line[offset : offset + depth]
            added = line if added is None else added + line
        out_ref[pl.ds(base, depth), 2 * width :] = added


def token_products(patches, embed_weight, cotangent):
    n, ndp = lax.axis_size("group"), lax.axis_size("dp")
    tok_rows, depth = patches.shape
    width = embed_weight.shape[1]
    parts = 128 // math.gcd(depth, 128)
    rows = tok_rows // parts
    packed = jnp.concatenate(
        [patches[q * rows : (q + 1) * rows] for q in range(parts)], axis=1
    )
    chunk = 256
    while rows % chunk:
        chunk //= 2
    chunks = rows // chunk
    hops = n // 2
    lanes = parts * depth
    window = max(window_of(q, depth)[1] for q in range(parts))
    anywhere = pl.BlockSpec(memory_space=pl.ANY)
    in_vmem = pl.BlockSpec(memory_space=pltpu.VMEM)
    ring = pltpu.SemaphoreType.DMA((hops, chunks))
    return pl.pallas_call(
        functools.partial(token_kernel, n, ndp, parts, depth, chunk),
        out_shape=(
            jax.ShapeDtypeStruct((n * depth, 2 * width + 128), jnp.float32),
            jax.ShapeDtypeStruct((width + 8, 2 * width), jnp.float32),
        ),
        in_specs=[anywhere] * 3,
        out_specs=(in_vmem, in_vmem),
        scratch_shapes=[
            pltpu.VMEM((n, rows, lanes), jnp.bfloat16),
            pltpu.VMEM((tok_rows, width), jnp.bfloat16),
            pltpu.VMEM((ndp,) + embed_weight.shape, jnp.bfloat16),
            pltpu.VMEM((n, parts, window, width), jnp.bfloat16),
            pltpu.VMEM((n, parts, 2 * width, window), jnp.float32),
            pltpu.VMEM((n, 8, lanes), jnp.float32),
            pltpu.VMEM((chunk, 2 * width), jnp.bfloat16),
            ring, ring, ring, ring,
            pltpu.SemaphoreType.DMA((ndp,)),
            pltpu.SemaphoreType.DMA((ndp,)),
            pltpu.SemaphoreType.DMA((3,)),
        ],
        compiler_params=pltpu.CompilerParams(
            collective_id=0, has_side_effects=True, vmem_limit_bytes=60 << 20
        ),
    )(packed, cotangent, embed_weight)


def body(patches, embed_weight, channel_gain, cotangent):
    tok_rows = patches.shape[0]
    total_tokens = tok_rows * lax.axis_size("dp")
    loss_scale = 1.0 / math.sqrt(total_tokens)
    identity = jnp.eye(GW, dtype=jnp.float32)
    width_here = embed_weight.shape[1]
    gain_here = lax.dynamic_slice_in_dim(
        channel_gain, lax.axis_index("group") * width_here, width_here
    )
    patch_products, stats = token_products(patches, embed_weight, cotangent)
    raw_products = block_diagonals(stats[:width_here, :width_here])
    cross = jnp.swapaxes(block_diagonals(stats[:width_here, width_here:]), 1, 2)
    sums = stats[width_here]
    raw_products, cross, sums = lax.psum((raw_products, cross, sums), "dp")
    patch_products = lax.psum_scatter(patch_products, "dp", scatter_dimension=0, tiled=True)
    return finish(
        raw_products, cross, sums, patch_products, gain_here, loss_scale, total_tokens, identity
    )


def finish(raw_products, cross, sums, patch_products, gain_here, loss_scale, total_tokens, identity):
    width_here = gain_here.shape[0]
    mean_groups = (sums[:width_here] / total_tokens).reshape(-1, GW)
    cot_sums = sums[width_here:].reshape(-1, GW)
    covariance = (
        raw_products / total_tokens
        - jnp.einsum("ga,gb->gab", mean_groups, mean_groups, precision=highest)
        + EPSILON * identity
    )
    whitener, pullback = jax.vjp(whiten_matrix, covariance)
    cross = loss_scale * (
        cross - jnp.einsum("ga,gb->gab", cot_sums, mean_groups, precision=highest)
    )
    gain_grad = jnp.sum(cross * whitener, axis=2).reshape(-1)
    scale = loss_scale * gain_here
    (grad_cov,) = pullback(cross * gain_here.reshape(-1, GW)[:, :, None])
    symmetric = (grad_cov + jnp.swapaxes(grad_cov, 1, 2)) / total_tokens
    patch_sums = patch_products[:, 2 * width_here : 2 * width_here + 1]
    rows = patch_products.shape[0]
    feat_part = patch_products[:, :width_here] - patch_sums * mean_groups.reshape(-1)
    cot_part = scale * (
        patch_products[:, width_here : 2 * width_here]
        - patch_sums * (cot_sums.reshape(-1) / total_tokens)
    )
    weight_grad = jnp.einsum(
        "rga,gab->rgb", cot_part.reshape(rows, -1, GW), whitener, precision=highest
    ) + jnp.einsum("rgb,gcb->rgc", feat_part.reshape(rows, -1, GW), symmetric, precision=highest)
    return (weight_grad.reshape(rows, -1), gain_grad)


def solution(mesh):
    placed = (P("dp", "group"), P("dp", "group"), P(), P("dp", "group"))
    return jax.shard_map(
        body, mesh=mesh, in_specs=placed, out_specs=(P("dp", "group"), P("group")), check_vma=False
    )
```

```python
import functools
import math

import jax
import jax.numpy as jnp
from jax import lax
from jax.experimental import pallas as pl
from jax.experimental.pallas import tpu as pltpu
from jax.sharding import PartitionSpec as P

GW = 64
ITERS = 5


EPSILON = 1e-05
highest = lax.Precision.HIGHEST


def matmul_batch(left, right):
    return jnp.einsum("gij,gjk->gik", left, right, precision=highest)


def whiten_matrix(covariance):
    width = covariance.shape[-1]
    traces = jnp.trace(covariance, axis1=1, axis2=2)
    normed = covariance / traces[:, None, None]
    iterate = jnp.broadcast_to(jnp.eye(width, dtype=jnp.float32), covariance.shape)
    for counter in range(ITERS):
        cubed = matmul_batch(matmul_batch(iterate, iterate), iterate)
        iterate = 1.5 * iterate - 0.5 * matmul_batch(cubed, normed)
    return iterate / jnp.sqrt(traces)[:, None, None]


MESH = pl.DeviceIdType.MESH
LEAD = 2


def window_of(part, depth):
    start = part * depth // 128 * 128
    stop = -(-(part + 1) * depth // 128) * 128
    return start, stop - start, part * depth - start


def token_kernel(
    n, ndp, parts, depth, chunk,
    x_hbm, cot_hbm, w_hbm,
    out_ref, stats_out, sums_out,
    stats_ref, packed_stats, stats_in, packed_sums, sums_in, products, products_in,
    held, cot, weights, padded, totals, patch_sums, bank,
    send_right, recv_right, send_left, recv_left, w_send, w_recv, local_sem,
    stats_send, stats_recv, sums_send, sums_recv, products_send, products_recv,
):
    me = lax.axis_index("group")
    mine = lax.axis_index("dp")
    right, left = lax.rem(me + 1, n), lax.rem(me + n - 1, n)
    rows = x_hbm.shape[0]
    chunks = rows // chunk
    width = cot.shape[1]
    hops = n // 2
    slab = w_hbm.shape[0]

    own_x = pltpu.make_async_copy(x_hbm, held.at[0], local_sem.at[0])
    own_cot = pltpu.make_async_copy(cot_hbm, cot, local_sem.at[1])
    own_w = pltpu.make_async_copy(w_hbm, weights.at[mine], local_sem.at[2])
    own_x.start()
    own_cot.start()
    own_w.start()

    barrier = pltpu.get_barrier_semaphore()
    for step in range(1, ndp):
        pl.semaphore_signal(
            barrier, inc=1, device_id={"dp": lax.rem(mine + step, ndp)}, device_id_type=MESH
        )
    for neighbour in (left, right):
        pl.semaphore_signal(barrier, inc=1, device_id={"group": neighbour}, device_id_type=MESH)
    pl.semaphore_wait(barrier, ndp + 1)

    def w_copy(step):
        return pltpu.make_async_remote_copy(
            src_ref=w_hbm,
            dst_ref=weights.at[mine],
            send_sem=w_send.at[step],
            recv_sem=w_recv.at[step],
            device_id={"dp": lax.rem(mine + step, ndp)},
            device_id_type=MESH,
        )

    def x_copy(hop, piece, to_right):
        start, size = pl.multiple_of(piece * chunk, chunk), chunk
        if n % 2 == 0 and hop == hops:
            size = chunk // 2
            if not to_right:
                start = start + size
        span = pl.ds(pl.multiple_of(start, size), size)
        source = x_hbm.at[span] if hop == 1 else held.at[hop - 1 if to_right else n - hop + 1, span]
        send, recv = (send_right, recv_right) if to_right else (send_left, recv_left)
        return pltpu.make_async_remote_copy(
            src_ref=source,
            dst_ref=held.at[hop if to_right else n - hop, span],
            send_sem=send.at[hop - 1, piece],
            recv_sem=recv.at[hop - 1, piece],
            device_id={"group": right if to_right else left},
            device_id_type=MESH,
        )

    for step in range(1, ndp):
        w_copy(step).start()
    for piece in range(min(LEAD, chunks)):
        for to_right in (True, False):
            x_copy(1, piece, to_right).start()

    totals[...] = jnp.zeros_like(totals)
    patch_sums[...] = jnp.zeros_like(patch_sums)
    stats_ref[...] = jnp.zeros_like(stats_ref)
    padded[...] = jnp.zeros_like(padded)
    own_w.wait()
    for step in range(1, ndp):
        w_copy(step).wait()
    per = depth // slab
    for j in range(n):
        for part in range(parts):
            offset = window_of(part, depth)[2]
            for k in range(per):
                padded[j, part, offset + k * slab : offset + (k + 1) * slab, :] = weights[
                    j * per + k
                ]
    own_x.wait()
    own_cot.wait()
    ones = jnp.ones((16, chunk), jnp.bfloat16)

    def compute(piece):
        span = pl.ds(pl.multiple_of(piece * chunk, chunk), chunk)
        for part in range(parts):
            start, size, _ = window_of(part, depth)
            embedded = jnp.zeros((chunk, width), jnp.float32)
            for slot in range(n):
                origin = lax.rem(me - slot + n, n)
                embedded += jnp.dot(
                    held[slot, span, start : start + size],
                    padded[origin, part, :size, :],
                    preferred_element_type=jnp.float32,
                )
            tokens = pl.ds(pl.multiple_of(part * rows + piece * chunk, chunk), chunk)
            bank[:, :width] = embedded.astype(jnp.bfloat16)
            bank[:, width:] = cot[tokens, :]
            both = bank[...]
            flipped = both.T
            stats_ref[:width, :] += jnp.dot(
                flipped[:width], both, preferred_element_type=jnp.float32
            )
            stats_ref[width:, :] += jnp.dot(ones, both, preferred_element_type=jnp.float32)[:8]
            for slot in range(n):
                totals[slot, part, :, :size] += jnp.dot(
                    flipped,
                    held[slot, span, start : start + size],
                    preferred_element_type=jnp.float32,
                )
        for slot in range(n):
            patch_sums[slot] += jnp.dot(
                ones, held[slot, span, :], preferred_element_type=jnp.float32
            )[:8]

    def arrive(hop, piece):
        for to_right in (True, False):
            x_copy(hop, piece, to_right).wait()

    @pl.loop(0, chunks + LEAD * (hops - 1))
    def _(step):
        @pl.when(step + LEAD < chunks)
        def _():
            for to_right in (True, False):
                x_copy(1, step + LEAD, to_right).start()

        for hop in range(1, hops):
            piece = step - LEAD * (hop - 1)

            @pl.when((piece >= 0) & (piece < chunks))
            def _():
                for to_right in (True, False):
                    x_copy(hop, piece, to_right).wait_recv()
                    x_copy(hop + 1, piece, to_right).start()

        piece = step - LEAD * (hops - 1)

        @pl.when(piece >= 0)
        def _():
            for to_right in (True, False):
                x_copy(hops, piece, to_right).wait_recv()
            compute(piece)

    @pl.loop(0, chunks)
    def _(piece):
        for hop in range(1, hops + 1):
            for to_right in (True, False):
                x_copy(hop, piece, to_right).wait_send()

    def exchange(source, landing, send, recv):
        return [
            pltpu.make_async_remote_copy(
                src_ref=source(lax.rem(mine + step, ndp)),
                dst_ref=landing.at[mine],
                send_sem=send.at[step],
                recv_sem=recv.at[step],
                device_id={"dp": lax.rem(mine + step, ndp)},
                device_id_type=MESH,
            )
            for step in range(1, ndp)
        ]

    lane_group = lax.rem(lax.broadcasted_iota(jnp.int32, (GW, 2 * width), 1), width) // GW
    diagonal = jnp.zeros((GW, 2 * width), jnp.float32)
    for g in range(width // GW):
        diagonal = jnp.where(lane_group == g, stats_ref[g * GW : (g + 1) * GW, :], diagonal)
    packed_stats[:GW, :] = diagonal
    packed_stats[GW:, :] = stats_ref[width:, :]
    packed_sums[...] = jnp.zeros_like(packed_sums)
    for slot in range(n):
        packed_sums[pl.ds(lax.rem(me - slot + n, n), 1), :] = patch_sums[slot, :1, :]
    stats_copies = exchange(lambda other: packed_stats, stats_in, stats_send, stats_recv)
    sums_copies = exchange(lambda other: packed_sums, sums_in, sums_send, sums_recv)
    for copy in stats_copies + sums_copies:
        copy.start()
    stats_in[mine] = packed_stats[...]
    sums_in[mine] = packed_sums[...]

    for slot in range(n):
        origin = lax.rem(me - slot + n, n)
        base = pl.multiple_of(origin * depth, 8)
        gathered = None
        for part in range(parts):
            start, size, offset = window_of(part, depth)
            block = totals[slot, part, :, :size].T[offset : offset + depth]
            gathered = block if gathered is None else gathered + block
        products[pl.ds(base, depth), :] = gathered
    product_copies = exchange(
        lambda other: products.at[pl.ds(pl.multiple_of(other * slab, 8), slab)],
        products_in,
        products_send,
        products_recv,
    )
    for copy in product_copies:
        copy.start()
    products_in[mine] = products[pl.ds(pl.multiple_of(mine * slab, 8), slab), :]
    for copy in stats_copies + sums_copies:
        copy.wait()
    stats_out[...] = sum(stats_in[k] for k in range(ndp))
    sums_out[...] = sum(sums_in[k] for k in range(ndp))
    for copy in product_copies:
        copy.wait()
    out_ref[...] = sum(products_in[k] for k in range(ndp))


def token_products(patches, embed_weight, cotangent):
    n, ndp = lax.axis_size("group"), lax.axis_size("dp")
    tok_rows, depth = patches.shape
    width = embed_weight.shape[1]
    parts = 128 // math.gcd(depth, 128)
    rows = tok_rows // parts
    packed = jnp.concatenate(
        [patches[q * rows : (q + 1) * rows] for q in range(parts)], axis=1
    )
    chunk = 256
    while rows % chunk:
        chunk //= 2
    chunks = rows // chunk
    hops = n // 2
    lanes = parts * depth
    window = max(window_of(q, depth)[1] for q in range(parts))
    anywhere = pl.BlockSpec(memory_space=pl.ANY)
    in_vmem = pl.BlockSpec(memory_space=pltpu.VMEM)
    slab = embed_weight.shape[0]
    stats_shape = (GW + 8, 2 * width)
    sums_shape = (-(-n // 8) * 8, lanes)
    peers = pltpu.SemaphoreType.DMA((ndp,))
    ring = pltpu.SemaphoreType.DMA((hops, chunks))
    return pl.pallas_call(
        functools.partial(token_kernel, n, ndp, parts, depth, chunk),
        out_shape=(
            jax.ShapeDtypeStruct((slab, 2 * width), jnp.float32),
            jax.ShapeDtypeStruct(stats_shape, jnp.float32),
            jax.ShapeDtypeStruct(sums_shape, jnp.float32),
        ),
        in_specs=[anywhere] * 3,
        out_specs=(in_vmem,) * 3,
        scratch_shapes=[
            pltpu.VMEM((width + 8, 2 * width), jnp.float32),
            pltpu.VMEM(stats_shape, jnp.float32),
            pltpu.VMEM((ndp,) + stats_shape, jnp.float32),
            pltpu.VMEM(sums_shape, jnp.float32),
            pltpu.VMEM((ndp,) + sums_shape, jnp.float32),
            pltpu.VMEM((n * depth, 2 * width), jnp.float32),
            pltpu.VMEM((ndp, slab, 2 * width), jnp.float32),
            pltpu.VMEM((n, rows, lanes), jnp.bfloat16),
            pltpu.VMEM((tok_rows, width), jnp.bfloat16),
            pltpu.VMEM((ndp,) + embed_weight.shape, jnp.bfloat16),
            pltpu.VMEM((n, parts, window, width), jnp.bfloat16),
            pltpu.VMEM((n, parts, 2 * width, window), jnp.float32),
            pltpu.VMEM((n, 8, lanes), jnp.float32),
            pltpu.VMEM((chunk, 2 * width), jnp.bfloat16),
            ring, ring, ring, ring,
            peers, peers,
            pltpu.SemaphoreType.DMA((3,)),
            peers, peers, peers, peers, peers, peers,
        ],
        compiler_params=pltpu.CompilerParams(
            collective_id=0, has_side_effects=True, vmem_limit_bytes=60 << 20
        ),
    )(packed, cotangent, embed_weight)


def body(patches, embed_weight, channel_gain, cotangent):
    tok_rows = patches.shape[0]
    total_tokens = tok_rows * lax.axis_size("dp")
    loss_scale = 1.0 / math.sqrt(total_tokens)
    identity = jnp.eye(GW, dtype=jnp.float32)
    width_here = embed_weight.shape[1]
    gain_here = lax.dynamic_slice_in_dim(
        channel_gain, lax.axis_index("group") * width_here, width_here
    )
    patch_products, stats, packed_sums = token_products(patches, embed_weight, cotangent)
    n, depth, slab = lax.axis_size("group"), patches.shape[1], embed_weight.shape[0]
    raw_products = stats[:GW, :width_here].reshape(GW, -1, GW).transpose(1, 0, 2)
    cross = stats[:GW, width_here:].reshape(GW, -1, GW).transpose(1, 2, 0)
    sums = stats[GW]
    patch_sums = jnp.sum(packed_sums[:n].reshape(n, -1, depth), axis=1).reshape(-1)
    patch_sums = lax.dynamic_slice_in_dim(patch_sums, lax.axis_index("dp") * slab, slab)[:, None]
    return finish(
        raw_products, cross, sums, patch_products, patch_sums,
        gain_here, loss_scale, total_tokens, identity,
    )


def finish(
    raw_products, cross, sums, patch_products, patch_sums,
    gain_here, loss_scale, total_tokens, identity,
):
    width_here = gain_here.shape[0]
    mean_groups = (sums[:width_here] / total_tokens).reshape(-1, GW)
    cot_sums = sums[width_here:].reshape(-1, GW)
    covariance = (
        raw_products / total_tokens
        - jnp.einsum("ga,gb->gab", mean_groups, mean_groups, precision=highest)
        + EPSILON * identity
    )
    whitener, pullback = jax.vjp(whiten_matrix, covariance)
    cross = loss_scale * (
        cross - jnp.einsum("ga,gb->gab", cot_sums, mean_groups, precision=highest)
    )
    gain_grad = jnp.sum(cross * whitener, axis=2).reshape(-1)
    scale = loss_scale * gain_here
    (grad_cov,) = pullback(cross * gain_here.reshape(-1, GW)[:, :, None])
    symmetric = (grad_cov + jnp.swapaxes(grad_cov, 1, 2)) / total_tokens
    rows = patch_products.shape[0]
    feat_part = patch_products[:, :width_here] - patch_sums * mean_groups.reshape(-1)
    cot_part = scale * (
        patch_products[:, width_here : 2 * width_here]
        - patch_sums * (cot_sums.reshape(-1) / total_tokens)
    )
    weight_grad = jnp.einsum(
        "rga,gab->rgb", cot_part.reshape(rows, -1, GW), whitener, precision=highest
    ) + jnp.einsum("rgb,gcb->rgc", feat_part.reshape(rows, -1, GW), symmetric, precision=highest)
    return (weight_grad.reshape(rows, -1), gain_grad)


def solution(mesh):
    placed = (P("dp", "group"), P("dp", "group"), P(), P("dp", "group"))
    return jax.shard_map(
        body, mesh=mesh, in_specs=placed, out_specs=(P("dp", "group"), P("group")), check_vma=False
    )
```

```python
import functools
import math

import jax
import jax.numpy as jnp
from jax import lax
from jax.experimental import pallas as pl
from jax.experimental.pallas import tpu as pltpu
from jax.sharding import PartitionSpec as P

GW = 64
ITERS = 5


EPSILON = 1e-05
highest = lax.Precision.HIGHEST


def matmul_batch(left, right):
    return jnp.einsum("gij,gjk->gik", left, right, precision=highest)


def whiten_matrix(covariance):
    width = covariance.shape[-1]
    traces = jnp.trace(covariance, axis1=1, axis2=2)
    normed = covariance / traces[:, None, None]
    iterate = jnp.broadcast_to(jnp.eye(width, dtype=jnp.float32), covariance.shape)
    for counter in range(ITERS):
        cubed = matmul_batch(matmul_batch(iterate, iterate), iterate)
        iterate = 1.5 * iterate - 0.5 * matmul_batch(cubed, normed)
    return iterate / jnp.sqrt(traces)[:, None, None]


MESH = pl.DeviceIdType.MESH
LEAD = 2


def window_of(part, depth):
    start = part * depth // 128 * 128
    stop = -(-(part + 1) * depth // 128) * 128
    return start, stop - start, part * depth - start


def token_kernel(
    n, ndp, parts, depth, chunk,
    x_hbm, cot_hbm, w_hbm,
    out_ref, stats_out, sums_out,
    stats_ref, packed_stats, stats_in, packed_sums, sums_in, products, products_in,
    held, cot, weights, padded, totals, patch_sums, bank,
    send_right, recv_right, send_left, recv_left, w_send, w_recv, local_sem,
    stats_send, stats_recv, sums_send, sums_recv, products_send, products_recv,
):
    me = lax.axis_index("group")
    mine = lax.axis_index("dp")
    right, left = lax.rem(me + 1, n), lax.rem(me + n - 1, n)
    rows = x_hbm.shape[0]
    chunks = rows // chunk
    width = cot.shape[1]
    hops = n // 2
    slab = w_hbm.shape[0]

    own_x = pltpu.make_async_copy(x_hbm, held.at[0], local_sem.at[0])
    own_cot = pltpu.make_async_copy(cot_hbm, cot, local_sem.at[1])
    own_w = pltpu.make_async_copy(w_hbm, weights.at[mine], local_sem.at[2])
    own_x.start()
    own_cot.start()
    own_w.start()

    barrier = pltpu.get_barrier_semaphore()
    for step in range(1, ndp):
        pl.semaphore_signal(
            barrier, inc=1, device_id={"dp": lax.rem(mine + step, ndp)}, device_id_type=MESH
        )
    for neighbour in (left, right):
        pl.semaphore_signal(barrier, inc=1, device_id={"group": neighbour}, device_id_type=MESH)
    pl.semaphore_wait(barrier, ndp + 1)

    def w_copy(step):
        return pltpu.make_async_remote_copy(
            src_ref=w_hbm,
            dst_ref=weights.at[mine],
            send_sem=w_send.at[step],
            recv_sem=w_recv.at[step],
            device_id={"dp": lax.rem(mine + step, ndp)},
            device_id_type=MESH,
        )

    def x_copy(hop, piece, to_right):
        start, size = pl.multiple_of(piece * chunk, chunk), chunk
        if n % 2 == 0 and hop == hops:
            size = chunk // 2
            if not to_right:
                start = start + size
        span = pl.ds(pl.multiple_of(start, size), size)
        source = x_hbm.at[span] if hop == 1 else held.at[hop - 1 if to_right else n - hop + 1, span]
        send, recv = (send_right, recv_right) if to_right else (send_left, recv_left)
        return pltpu.make_async_remote_copy(
            src_ref=source,
            dst_ref=held.at[hop if to_right else n - hop, span],
            send_sem=send.at[hop - 1, piece],
            recv_sem=recv.at[hop - 1, piece],
            device_id={"group": right if to_right else left},
            device_id_type=MESH,
        )

    for step in range(1, ndp):
        w_copy(step).start()
    for piece in range(min(LEAD, chunks)):
        for to_right in (True, False):
            x_copy(1, piece, to_right).start()

    totals[...] = jnp.zeros_like(totals)
    patch_sums[...] = jnp.zeros_like(patch_sums)
    stats_ref[...] = jnp.zeros_like(stats_ref)
    padded[...] = jnp.zeros_like(padded)
    own_w.wait()
    for step in range(1, ndp):
        w_copy(step).wait()
    per = depth // slab
    for j in range(n):
        for part in range(parts):
            offset = window_of(part, depth)[2]
            for k in range(per):
                padded[j, part, offset + k * slab : offset + (k + 1) * slab, :] = weights[
                    j * per + k
                ]
    own_x.wait()
    own_cot.wait()
    ones = jnp.ones((16, chunk), jnp.bfloat16)

    def compute(piece):
        span = pl.ds(pl.multiple_of(piece * chunk, chunk), chunk)
        for part in range(parts):
            start, size, _ = window_of(part, depth)
            embedded = jnp.zeros((chunk, width), jnp.float32)
            for slot in range(n):
                origin = lax.rem(me - slot + n, n)
                embedded += jnp.dot(
                    held[slot, span, start : start + size],
                    padded[origin, part, :size, :],
                    preferred_element_type=jnp.float32,
                )
            tokens = pl.ds(pl.multiple_of(part * rows + piece * chunk, chunk), chunk)
            bank[:, :width] = embedded.astype(jnp.bfloat16)
            bank[:, width:] = cot[tokens, :]
            both = bank[...]
            flipped = both.T
            stats_ref[:width, :] += jnp.dot(
                flipped[:width], both, preferred_element_type=jnp.float32
            )
            stats_ref[width:, :] += jnp.dot(ones, both, preferred_element_type=jnp.float32)[:8]
            for slot in range(n):
                totals[slot, part, :, :size] += jnp.dot(
                    flipped,
                    held[slot, span, start : start + size],
                    preferred_element_type=jnp.float32,
                )
        for slot in range(n):
            patch_sums[slot] += jnp.dot(
                ones, held[slot, span, :], preferred_element_type=jnp.float32
            )[:8]

    def arrive(hop, piece):
        for to_right in (True, False):
            x_copy(hop, piece, to_right).wait()

    @pl.loop(0, chunks + LEAD * (hops - 1))
    def _(step):
        @pl.when(step + LEAD < chunks)
        def _():
            for to_right in (True, False):
                x_copy(1, step + LEAD, to_right).start()

        for hop in range(1, hops):
            piece = step - LEAD * (hop - 1)

            @pl.when((piece >= 0) & (piece < chunks))
            def _():
                for to_right in (True, False):
                    x_copy(hop, piece, to_right).wait_recv()
                    x_copy(hop + 1, piece, to_right).start()

        piece = step - LEAD * (hops - 1)

        @pl.when(piece >= 0)
        def _():
            for to_right in (True, False):
                x_copy(hops, piece, to_right).wait_recv()
            compute(piece)

    @pl.loop(0, chunks)
    def _(piece):
        for hop in range(1, hops + 1):
            for to_right in (True, False):
                x_copy(hop, piece, to_right).wait_send()

    def exchange(source, landing, send, recv):
        return [
            pltpu.make_async_remote_copy(
                src_ref=source(lax.rem(mine + step, ndp)),
                dst_ref=landing.at[mine],
                send_sem=send.at[step],
                recv_sem=recv.at[step],
                device_id={"dp": lax.rem(mine + step, ndp)},
                device_id_type=MESH,
            )
            for step in range(1, ndp)
        ]

    lane_group = lax.rem(lax.broadcasted_iota(jnp.int32, (GW, 2 * width), 1), width) // GW
    diagonal = jnp.zeros((GW, 2 * width), jnp.float32)
    for g in range(width // GW):
        diagonal = jnp.where(lane_group == g, stats_ref[g * GW : (g + 1) * GW, :], diagonal)
    packed_stats[:GW, :] = diagonal
    packed_stats[GW:, :] = stats_ref[width:, :]
    packed_sums[...] = jnp.zeros_like(packed_sums)
    for slot in range(n):
        packed_sums[pl.ds(lax.rem(me - slot + n, n), 1), :] = patch_sums[slot, :1, :]
    stats_copies = exchange(lambda other: packed_stats, stats_in, stats_send, stats_recv)
    sums_copies = exchange(lambda other: packed_sums, sums_in, sums_send, sums_recv)
    for copy in stats_copies + sums_copies:
        copy.start()
    stats_in[mine] = packed_stats[...]
    sums_in[mine] = packed_sums[...]

    for slot in range(n):
        origin = lax.rem(me - slot + n, n)
        base = pl.multiple_of(origin * depth, 8)
        gathered = None
        for part in range(parts):
            start, size, offset = window_of(part, depth)
            block = totals[slot, part, :, :size].T[offset : offset + depth]
            gathered = block if gathered is None else gathered + block
        products[pl.ds(base, depth), :] = gathered
    product_copies = exchange(
        lambda other: products.at[pl.ds(pl.multiple_of(other * slab, 8), slab)],
        products_in,
        products_send,
        products_recv,
    )
    for copy in product_copies:
        copy.start()
    products_in[mine] = products[pl.ds(pl.multiple_of(mine * slab, 8), slab), :]
    for copy in stats_copies + sums_copies:
        copy.wait()
    stats_out[...] = sum(stats_in[k] for k in range(ndp))
    sums_out[...] = sum(sums_in[k] for k in range(ndp))
    for copy in product_copies:
        copy.wait()
    out_ref[...] = sum(products_in[k] for k in range(ndp))


def handed(piece, chunks):
    return (lax.rem(piece, 2) == 1) & (piece < 2 * (chunks * 5 // 13))


def line_kernel(
    n, ndp, parts, depth, chunk,
    x_hbm, cot_hbm, w_hbm,
    out_ref, stats_out, sums_out,
    stats, packed_stats, stats_in, packed_sums, sums_in, products, products_in,
    held, cot, weights, padded, totals, patch_sums, bank,
    mate_part, mate_stats, whole_sums, mate_products,
    own_send, own_recv, mid_send, mid_recv, pass_send, pass_recv,
    out1_send, out1_recv, out2_send, out2_recv, cot_send, cot_recv,
    w_send, w_recv, local_sem,
    stats_send, stats_recv, sums_send, sums_recv, products_send, products_recv,
    mate_send, mate_recv, last_send, last_recv,
):
    me = lax.axis_index("group")
    mine = lax.axis_index("dp")
    inner = (me == 1) | (me == 2)
    outer = (me == 0) | (me == 3)
    mate = me + 1 - 2 * lax.rem(me, 2)
    across = 3 - me
    beyond = 3 - mate
    rows = x_hbm.shape[0]
    chunks = rows // chunk
    width = w_hbm.shape[1]
    slab = w_hbm.shape[0]

    own_x = pltpu.make_async_copy(x_hbm, held.at[me], local_sem.at[0])
    own_cot = pltpu.make_async_copy(cot_hbm, cot.at[0], local_sem.at[1])
    own_w = pltpu.make_async_copy(w_hbm, weights.at[0, mine], local_sem.at[2])
    own_x.start()
    own_cot.start()
    own_w.start()

    barrier = pltpu.get_barrier_semaphore()
    for step in range(1, ndp):
        pl.semaphore_signal(
            barrier, inc=1, device_id={"dp": lax.rem(mine + step, ndp)}, device_id_type=MESH
        )
    pl.semaphore_signal(barrier, inc=1, device_id={"group": mate}, device_id_type=MESH)

    @pl.when(inner)
    def _():
        pl.semaphore_signal(barrier, inc=1, device_id={"group": across}, device_id_type=MESH)
        pl.semaphore_wait(barrier, ndp + 1)

    @pl.when(outer)
    def _():
        pl.semaphore_wait(barrier, ndp)

    def remote(source, target, send, recv, to):
        return pltpu.make_async_remote_copy(
            src_ref=source, dst_ref=target, send_sem=send, recv_sem=recv,
            device_id=to, device_id_type=MESH,
        )

    def w_copy(step):
        return remote(
            w_hbm, weights.at[0, mine], w_send.at[step], w_recv.at[step],
            {"dp": lax.rem(mine + step, ndp)},
        )

    def span_of(piece):
        return pl.ds(pl.multiple_of(piece * chunk, chunk), chunk)

    to_mate, to_across = {"group": mate}, {"group": across}

    def block(origin, piece, send, recv, to, own=False):
        span = span_of(piece)
        return remote(
            x_hbm.at[span] if own else held.at[origin, span],
            held.at[origin, span], send.at[piece], recv.at[piece], to,
        )

    def own_copy(piece):
        return block(me, piece, own_send, own_recv, to_mate, True)

    def mid_copy(piece):
        return block(me, piece, mid_send, mid_recv, to_across, True)

    def pass_copy(piece):
        return block(mate, piece, pass_send, pass_recv, to_across)

    def out1_copy(piece):
        return block(across, piece, out1_send, out1_recv, to_mate)

    def out2_copy(piece):
        return block(beyond, piece, out2_send, out2_recv, to_mate)

    def cot_copy(piece):
        span = span_of(piece)
        return remote(
            cot_hbm.at[:, span], cot.at[1, :, span], cot_send.at[piece], cot_recv.at[piece],
            to_mate,
        )

    mate_w = remote(weights.at[0], weights.at[1], mate_send.at[0], mate_recv.at[0], to_mate)
    mate_p = remote(mate_part, mate_products, last_send.at[0], last_recv.at[0], to_mate)
    mate_s = remote(packed_stats.at[1], mate_stats, mate_send.at[1], mate_recv.at[1], to_mate)
    mate_x = remote(whole_sums, sums_out, last_send.at[1], last_recv.at[1], to_mate)

    for step in range(1, ndp):
        w_copy(step).start()

    @pl.when(inner)
    def _():
        for piece in range(min(LEAD, chunks)):
            mid_copy(piece).start()

    @pl.when(outer)
    def _():
        for piece in range(min(LEAD, chunks)):
            own_copy(piece).start()

    totals[...] = jnp.zeros_like(totals)
    patch_sums[...] = jnp.zeros_like(patch_sums)
    stats[...] = jnp.zeros_like(stats)
    padded[...] = jnp.zeros_like(padded)
    own_w.wait()
    for step in range(1, ndp):
        w_copy(step).wait()
    per = depth // slab

    def pad_weights(which):
        for j in range(n):
            for part in range(parts):
                offset = window_of(part, depth)[2]
                for k in range(per):
                    padded[which, j, part, offset + k * slab : offset + (k + 1) * slab, :] = (
                        weights[which, j * per + k]
                    )

    @pl.when(outer)
    def _():
        mate_w.start()

        @pl.loop(0, chunks)
        def _(piece):
            @pl.when(piece >= LEAD)
            def _():
                own_copy(piece).start()

            @pl.when(handed(piece, chunks))
            def _():
                cot_copy(piece).start()

    pad_weights(0)
    own_x.wait()
    own_cot.wait()
    ones = jnp.ones((16, chunk), jnp.bfloat16)

    def compute(piece, which):
        span = span_of(piece)
        for part in range(parts):
            start, size, _ = window_of(part, depth)
            embedded = jnp.zeros((chunk, width), jnp.float32)
            for slot in range(n):
                embedded += jnp.dot(
                    held[slot, span, start : start + size],
                    padded[which, slot, part, :size, :],
                    preferred_element_type=jnp.float32,
                )
            bank[:, :width] = embedded.astype(jnp.bfloat16)
            bank[:, width:] = cot[which, part, span, :]
            both = bank[...]
            flipped = both.T
            stats[which, :width, :] += jnp.dot(
                flipped[:width], both, preferred_element_type=jnp.float32
            )
            stats[which, width:, :] += jnp.dot(ones, both, preferred_element_type=jnp.float32)[:8]
            for slot in range(n):
                totals[which, slot, part, :, :size] += jnp.dot(
                    flipped,
                    held[slot, span, start : start + size],
                    preferred_element_type=jnp.float32,
                )

    def add_sums(piece):
        for slot in range(n):
            patch_sums[slot] += jnp.dot(
                ones, held[slot, span_of(piece), :], preferred_element_type=jnp.float32
            )[:8]

    def exchange(source, landing, send, recv):
        return [
            remote(
                source(lax.rem(mine + step, ndp)), landing.at[mine],
                send.at[step], recv.at[step], {"dp": lax.rem(mine + step, ndp)},
            )
            for step in range(1, ndp)
        ]

    def product_copies(which):
        return exchange(
            lambda other: products.at[which, pl.ds(pl.multiple_of(other * slab, 8), slab)],
            products_in.at[which], products_send.at[which], products_recv.at[which],
        )

    lane_group = lax.rem(lax.broadcasted_iota(jnp.int32, (GW, 2 * width), 1), width) // GW

    def pack_stats(which):
        diagonal = jnp.zeros((GW, 2 * width), jnp.float32)
        for g in range(width // GW):
            diagonal = jnp.where(
                lane_group == g, stats[which, g * GW : (g + 1) * GW, :], diagonal
            )
        packed_stats[which, :GW, :] = diagonal
        packed_stats[which, GW:, :] = stats[which, width:, :]

    def send_products(which):
        for slot in range(n):
            gathered = None
            for part in range(parts):
                start, size, offset = window_of(part, depth)
                rows_here = totals[which, slot, part, :, :size].T[offset : offset + depth]
                gathered = rows_here if gathered is None else gathered + rows_here
            products[which, slot * depth : (slot + 1) * depth, :] = gathered
        for copy in product_copies(which):
            copy.start()
        products_in[which, mine] = products[
            which, pl.ds(pl.multiple_of(mine * slab, 8), slab), :
        ]

    given = 2 * (chunks * 5 // 13)

    @pl.when(inner)
    def _():
        @pl.loop(0, chunks + LEAD)
        def _(step):
            @pl.when(step + LEAD < chunks)
            def _():
                mid_copy(step + LEAD).start()

            @pl.when(step < chunks)
            def _():
                own_copy(step).wait_recv()
                pass_copy(step).start()
                mid_copy(step).wait_recv()

                @pl.when(jnp.logical_not(handed(step, chunks)))
                def _():
                    own_copy(step).start()
                    out1_copy(step).start()

            @pl.when(step == LEAD)
            def _():
                mate_w.wait_recv()
                pad_weights(1)

            piece = step - LEAD

            @pl.when(piece >= 0)
            def _():
                pass_copy(piece).wait_recv()

                @pl.when(jnp.logical_not(handed(piece, chunks)))
                def _():
                    out2_copy(piece).start()

                compute(piece, 0)
                add_sums(piece)

                @pl.when(handed(piece, chunks))
                def _():
                    cot_copy(piece).wait_recv()
                    compute(piece, 1)

            @pl.when(piece == given)
            def _():
                pack_stats(1)
                mate_s.start()
                send_products(1)

    @pl.when(outer)
    def _():
        @pl.loop(0, chunks)
        def _(piece):
            @pl.when(jnp.logical_not(handed(piece, chunks)))
            def _():
                own_copy(piece).wait_recv()
                out1_copy(piece).wait_recv()
                out2_copy(piece).wait_recv()
                compute(piece, 0)

        mate_s.wait_recv()

    pack_stats(0)

    @pl.when(outer)
    def _():
        packed_stats[0] = packed_stats[0] + mate_stats[...]

    packed_sums[...] = jnp.zeros_like(packed_sums)
    for slot in range(n):
        packed_sums[slot : slot + 1, :] = patch_sums[slot, :1, :]
    stats_copies = exchange(lambda other: packed_stats.at[0], stats_in, stats_send, stats_recv)
    sums_copies = exchange(lambda other: packed_sums, sums_in, sums_send, sums_recv)
    for copy in sums_copies + stats_copies:
        copy.start()
    stats_in[mine] = packed_stats[0]
    sums_in[mine] = packed_sums[...]
    send_products(0)

    @pl.when(inner)
    def _():
        for copy in product_copies(1):
            copy.wait()
        mate_part[...] = sum(products_in[1, k] for k in range(ndp))
        mate_p.start()

    for copy in sums_copies:
        copy.wait()
    whole_sums[...] = sum(sums_in[k] for k in range(ndp))

    @pl.when(inner)
    def _():
        mate_x.start()
        sums_out[...] = whole_sums[...]

    for copy in stats_copies:
        copy.wait()
    stats_out[...] = sum(stats_in[k] for k in range(ndp))

    @pl.loop(0, chunks)
    def _(piece):
        @pl.when(inner)
        def _():
            mid_copy(piece).wait_send()
            pass_copy(piece).wait_send()

            @pl.when(jnp.logical_not(handed(piece, chunks)))
            def _():
                own_copy(piece).wait_send()
                out1_copy(piece).wait_send()
                out2_copy(piece).wait_send()

        @pl.when(outer)
        def _():
            own_copy(piece).wait_send()

            @pl.when(handed(piece, chunks))
            def _():
                cot_copy(piece).wait_send()

    for copy in product_copies(0):
        copy.wait()
    out_ref[...] = sum(products_in[0, k] for k in range(ndp))

    @pl.when(inner)
    def _():
        mate_s.wait_send()
        mate_p.wait_send()
        mate_x.wait_send()

    @pl.when(outer)
    def _():
        mate_w.wait_send()
        mate_x.wait_recv()
        mate_p.wait_recv()
        out_ref[...] = out_ref[...] + mate_products[...]


def line_products(packed, cotangent, embed_weight, parts, depth, chunk, stats_shape, sums_shape):
    n, ndp = lax.axis_size("group"), lax.axis_size("dp")
    rows, lanes = packed.shape
    slab, width = embed_weight.shape
    chunks = rows // chunk
    window = max(window_of(q, depth)[1] for q in range(parts))
    anywhere = pl.BlockSpec(memory_space=pl.ANY)
    in_vmem = pl.BlockSpec(memory_space=pltpu.VMEM)
    pieces = pltpu.SemaphoreType.DMA((chunks,))
    peers = pltpu.SemaphoreType.DMA((ndp,))
    pair = pltpu.SemaphoreType.DMA((2,))
    both_peers = pltpu.SemaphoreType.DMA((2, ndp))
    return pl.pallas_call(
        functools.partial(line_kernel, n, ndp, parts, depth, chunk),
        out_shape=(
            jax.ShapeDtypeStruct((slab, 2 * width), jnp.float32),
            jax.ShapeDtypeStruct(stats_shape, jnp.float32),
            jax.ShapeDtypeStruct(sums_shape, jnp.float32),
        ),
        in_specs=[anywhere] * 3,
        out_specs=(in_vmem,) * 3,
        scratch_shapes=[
            pltpu.VMEM((2, width + 8, 2 * width), jnp.float32),
            pltpu.VMEM((2,) + stats_shape, jnp.float32),
            pltpu.VMEM((ndp,) + stats_shape, jnp.float32),
            pltpu.VMEM(sums_shape, jnp.float32),
            pltpu.VMEM((ndp,) + sums_shape, jnp.float32),
            pltpu.VMEM((2, n * depth, 2 * width), jnp.float32),
            pltpu.VMEM((2, ndp, slab, 2 * width), jnp.float32),
            pltpu.VMEM((n, rows, lanes), jnp.bfloat16),
            pltpu.VMEM((2, parts, rows, width), jnp.bfloat16),
            pltpu.VMEM((2, ndp, slab, width), jnp.bfloat16),
            pltpu.VMEM((2, n, parts, window, width), jnp.bfloat16),
            pltpu.VMEM((2, n, parts, 2 * width, window), jnp.float32),
            pltpu.VMEM((n, 8, lanes), jnp.float32),
            pltpu.VMEM((chunk, 2 * width), jnp.bfloat16),
            pltpu.VMEM((slab, 2 * width), jnp.float32),
            pltpu.VMEM(stats_shape, jnp.float32),
            pltpu.VMEM(sums_shape, jnp.float32),
            pltpu.VMEM((slab, 2 * width), jnp.float32),
            *[pieces] * 12,
            peers, peers,
            pltpu.SemaphoreType.DMA((3,)),
            peers, peers, peers, peers, both_peers, both_peers,
            pair, pair, pair, pair,
        ],
        compiler_params=pltpu.CompilerParams(
            collective_id=1, has_side_effects=True, vmem_limit_bytes=60 << 20
        ),
    )(packed, cotangent.reshape(parts, rows, width), embed_weight)


def token_products(patches, embed_weight, cotangent):
    n, ndp = lax.axis_size("group"), lax.axis_size("dp")
    tok_rows, depth = patches.shape
    width = embed_weight.shape[1]
    parts = 128 // math.gcd(depth, 128)
    rows = tok_rows // parts
    packed = jnp.concatenate(
        [patches[q * rows : (q + 1) * rows] for q in range(parts)], axis=1
    )
    chunk = 256
    while rows % chunk:
        chunk //= 2
    chunks = rows // chunk
    hops = n // 2
    lanes = parts * depth
    window = max(window_of(q, depth)[1] for q in range(parts))
    anywhere = pl.BlockSpec(memory_space=pl.ANY)
    in_vmem = pl.BlockSpec(memory_space=pltpu.VMEM)
    slab = embed_weight.shape[0]
    stats_shape = (GW + 8, 2 * width)
    sums_shape = (-(-n // 8) * 8, lanes)
    peers = pltpu.SemaphoreType.DMA((ndp,))
    if n == 4 and 3 <= chunks:
        return line_products(
            packed, cotangent, embed_weight, parts, depth, chunk, stats_shape, sums_shape
        )
    ring = pltpu.SemaphoreType.DMA((hops, chunks))
    return pl.pallas_call(
        functools.partial(token_kernel, n, ndp, parts, depth, chunk),
        out_shape=(
            jax.ShapeDtypeStruct((slab, 2 * width), jnp.float32),
            jax.ShapeDtypeStruct(stats_shape, jnp.float32),
            jax.ShapeDtypeStruct(sums_shape, jnp.float32),
        ),
        in_specs=[anywhere] * 3,
        out_specs=(in_vmem,) * 3,
        scratch_shapes=[
            pltpu.VMEM((width + 8, 2 * width), jnp.float32),
            pltpu.VMEM(stats_shape, jnp.float32),
            pltpu.VMEM((ndp,) + stats_shape, jnp.float32),
            pltpu.VMEM(sums_shape, jnp.float32),
            pltpu.VMEM((ndp,) + sums_shape, jnp.float32),
            pltpu.VMEM((n * depth, 2 * width), jnp.float32),
            pltpu.VMEM((ndp, slab, 2 * width), jnp.float32),
            pltpu.VMEM((n, rows, lanes), jnp.bfloat16),
            pltpu.VMEM((tok_rows, width), jnp.bfloat16),
            pltpu.VMEM((ndp,) + embed_weight.shape, jnp.bfloat16),
            pltpu.VMEM((n, parts, window, width), jnp.bfloat16),
            pltpu.VMEM((n, parts, 2 * width, window), jnp.float32),
            pltpu.VMEM((n, 8, lanes), jnp.float32),
            pltpu.VMEM((chunk, 2 * width), jnp.bfloat16),
            ring, ring, ring, ring,
            peers, peers,
            pltpu.SemaphoreType.DMA((3,)),
            peers, peers, peers, peers, peers, peers,
        ],
        compiler_params=pltpu.CompilerParams(
            collective_id=0, has_side_effects=True, vmem_limit_bytes=60 << 20
        ),
    )(packed, cotangent, embed_weight)


def body(patches, embed_weight, channel_gain, cotangent):
    tok_rows = patches.shape[0]
    total_tokens = tok_rows * lax.axis_size("dp")
    loss_scale = 1.0 / math.sqrt(total_tokens)
    identity = jnp.eye(GW, dtype=jnp.float32)
    width_here = embed_weight.shape[1]
    gain_here = lax.dynamic_slice_in_dim(
        channel_gain, lax.axis_index("group") * width_here, width_here
    )
    patch_products, stats, packed_sums = token_products(patches, embed_weight, cotangent)
    n, depth, slab = lax.axis_size("group"), patches.shape[1], embed_weight.shape[0]
    raw_products = stats[:GW, :width_here].reshape(GW, -1, GW).transpose(1, 0, 2)
    cross = stats[:GW, width_here:].reshape(GW, -1, GW).transpose(1, 2, 0)
    sums = stats[GW]
    patch_sums = jnp.sum(packed_sums[:n].reshape(n, -1, depth), axis=1).reshape(-1)
    patch_sums = lax.dynamic_slice_in_dim(patch_sums, lax.axis_index("dp") * slab, slab)[:, None]
    return finish(
        raw_products, cross, sums, patch_products, patch_sums,
        gain_here, loss_scale, total_tokens, identity,
    )


def finish(
    raw_products, cross, sums, patch_products, patch_sums,
    gain_here, loss_scale, total_tokens, identity,
):
    width_here = gain_here.shape[0]
    mean_groups = (sums[:width_here] / total_tokens).reshape(-1, GW)
    cot_sums = sums[width_here:].reshape(-1, GW)
    covariance = (
        raw_products / total_tokens
        - jnp.einsum("ga,gb->gab", mean_groups, mean_groups, precision=highest)
        + EPSILON * identity
    )
    whitener, pullback = jax.vjp(whiten_matrix, covariance)
    cross = loss_scale * (
        cross - jnp.einsum("ga,gb->gab", cot_sums, mean_groups, precision=highest)
    )
    gain_grad = jnp.sum(cross * whitener, axis=2).reshape(-1)
    scale = loss_scale * gain_here
    (grad_cov,) = pullback(cross * gain_here.reshape(-1, GW)[:, :, None])
    symmetric = (grad_cov + jnp.swapaxes(grad_cov, 1, 2)) / total_tokens
    rows = patch_products.shape[0]
    feat_part = patch_products[:, :width_here] - patch_sums * mean_groups.reshape(-1)
    cot_part = scale * (
        patch_products[:, width_here : 2 * width_here]
        - patch_sums * (cot_sums.reshape(-1) / total_tokens)
    )
    weight_grad = jnp.einsum(
        "rga,gab->rgb", cot_part.reshape(rows, -1, GW), whitener, precision=highest
    ) + jnp.einsum("rgb,gcb->rgc", feat_part.reshape(rows, -1, GW), symmetric, precision=highest)
    return (weight_grad.reshape(rows, -1), gain_grad)


def solution(mesh):
    placed = (P("dp", "group"), P("dp", "group"), P(), P("dp", "group"))
    return jax.shard_map(
        body, mesh=mesh, in_specs=placed, out_specs=(P("dp", "group"), P("group")), check_vma=False
    )
```

```python
import functools
import math

import jax
import jax.numpy as jnp
from jax import lax
from jax.experimental import pallas as pl
from jax.experimental.pallas import tpu as pltpu
from jax.sharding import PartitionSpec as P

GW = 64
ITERS = 5


EPSILON = 1e-05
highest = lax.Precision.HIGHEST


def matmul_batch(left, right):
    return jnp.einsum("gij,gjk->gik", left, right, precision=highest)


def whiten_matrix(covariance):
    width = covariance.shape[-1]
    traces = jnp.trace(covariance, axis1=1, axis2=2)
    normed = covariance / traces[:, None, None]
    iterate = jnp.broadcast_to(jnp.eye(width, dtype=jnp.float32), covariance.shape)
    for counter in range(ITERS):
        cubed = matmul_batch(matmul_batch(iterate, iterate), iterate)
        iterate = 1.5 * iterate - 0.5 * matmul_batch(cubed, normed)
    return iterate / jnp.sqrt(traces)[:, None, None]


MESH = pl.DeviceIdType.MESH
LEAD = 2


def window_of(part, depth):
    start = part * depth // 128 * 128
    stop = -(-(part + 1) * depth // 128) * 128
    return start, stop - start, part * depth - start


def token_kernel(
    n, ndp, parts, depth, chunk,
    x_hbm, cot_hbm, w_hbm,
    out_ref, stats_out, sums_out,
    stats_ref, packed_stats, stats_in, packed_sums, sums_in, products, products_in,
    held, cot, weights, padded, totals, patch_sums, bank,
    send_right, recv_right, send_left, recv_left, w_send, w_recv, local_sem,
    stats_send, stats_recv, sums_send, sums_recv, products_send, products_recv,
):
    me = lax.axis_index("group")
    mine = lax.axis_index("dp")
    right, left = lax.rem(me + 1, n), lax.rem(me + n - 1, n)
    rows = x_hbm.shape[0]
    chunks = rows // chunk
    width = cot.shape[1]
    hops = n // 2
    slab = w_hbm.shape[0]

    own_x = pltpu.make_async_copy(x_hbm, held.at[0], local_sem.at[0])
    own_cot = pltpu.make_async_copy(cot_hbm, cot, local_sem.at[1])
    own_w = pltpu.make_async_copy(w_hbm, weights.at[mine], local_sem.at[2])
    own_x.start()
    own_cot.start()
    own_w.start()

    barrier = pltpu.get_barrier_semaphore()
    for step in range(1, ndp):
        pl.semaphore_signal(
            barrier, inc=1, device_id={"dp": lax.rem(mine + step, ndp)}, device_id_type=MESH
        )
    for neighbour in (left, right):
        pl.semaphore_signal(barrier, inc=1, device_id={"group": neighbour}, device_id_type=MESH)
    pl.semaphore_wait(barrier, ndp + 1)

    def w_copy(step):
        return pltpu.make_async_remote_copy(
            src_ref=w_hbm,
            dst_ref=weights.at[mine],
            send_sem=w_send.at[step],
            recv_sem=w_recv.at[step],
            device_id={"dp": lax.rem(mine + step, ndp)},
            device_id_type=MESH,
        )

    def x_copy(hop, piece, to_right):
        start, size = pl.multiple_of(piece * chunk, chunk), chunk
        if n % 2 == 0 and hop == hops:
            size = chunk // 2
            if not to_right:
                start = start + size
        span = pl.ds(pl.multiple_of(start, size), size)
        source = x_hbm.at[span] if hop == 1 else held.at[hop - 1 if to_right else n - hop + 1, span]
        send, recv = (send_right, recv_right) if to_right else (send_left, recv_left)
        return pltpu.make_async_remote_copy(
            src_ref=source,
            dst_ref=held.at[hop if to_right else n - hop, span],
            send_sem=send.at[hop - 1, piece],
            recv_sem=recv.at[hop - 1, piece],
            device_id={"group": right if to_right else left},
            device_id_type=MESH,
        )

    for step in range(1, ndp):
        w_copy(step).start()
    for piece in range(min(LEAD, chunks)):
        for to_right in (True, False):
            x_copy(1, piece, to_right).start()

    totals[...] = jnp.zeros_like(totals)
    patch_sums[...] = jnp.zeros_like(patch_sums)
    stats_ref[...] = jnp.zeros_like(stats_ref)
    padded[...] = jnp.zeros_like(padded)
    own_w.wait()
    for step in range(1, ndp):
        w_copy(step).wait()
    per = depth // slab
    for j in range(n):
        for part in range(parts):
            offset = window_of(part, depth)[2]
            for k in range(per):
                padded[j, part, offset + k * slab : offset + (k + 1) * slab, :] = weights[
                    j * per + k
                ]
    own_x.wait()
    own_cot.wait()
    ones = jnp.ones((16, chunk), jnp.bfloat16)

    def compute(piece):
        span = pl.ds(pl.multiple_of(piece * chunk, chunk), chunk)
        for part in range(parts):
            start, size, _ = window_of(part, depth)
            embedded = jnp.zeros((chunk, width), jnp.float32)
            for slot in range(n):
                origin = lax.rem(me - slot + n, n)
                embedded += jnp.dot(
                    held[slot, span, start : start + size],
                    padded[origin, part, :size, :],
                    preferred_element_type=jnp.float32,
                )
            tokens = pl.ds(pl.multiple_of(part * rows + piece * chunk, chunk), chunk)
            bank[:, :width] = embedded.astype(jnp.bfloat16)
            bank[:, width:] = cot[tokens, :]
            both = bank[...]
            flipped = both.T
            stats_ref[:width, :] += jnp.dot(
                flipped[:width], both, preferred_element_type=jnp.float32
            )
            stats_ref[width:, :] += jnp.dot(ones, both, preferred_element_type=jnp.float32)[:8]
            for slot in range(n):
                totals[slot, part, :, :size] += jnp.dot(
                    flipped,
                    held[slot, span, start : start + size],
                    preferred_element_type=jnp.float32,
                )
        for slot in range(n):
            patch_sums[slot] += jnp.dot(
                ones, held[slot, span, :], preferred_element_type=jnp.float32
            )[:8]

    def arrive(hop, piece):
        for to_right in (True, False):
            x_copy(hop, piece, to_right).wait()

    @pl.loop(0, chunks + LEAD * (hops - 1))
    def _(step):
        @pl.when(step + LEAD < chunks)
        def _():
            for to_right in (True, False):
                x_copy(1, step + LEAD, to_right).start()

        for hop in range(1, hops):
            piece = step - LEAD * (hop - 1)

            @pl.when((piece >= 0) & (piece < chunks))
            def _():
                for to_right in (True, False):
                    x_copy(hop, piece, to_right).wait_recv()
                    x_copy(hop + 1, piece, to_right).start()

        piece = step - LEAD * (hops - 1)

        @pl.when(piece >= 0)
        def _():
            for to_right in (True, False):
                x_copy(hops, piece, to_right).wait_recv()
            compute(piece)

    @pl.loop(0, chunks)
    def _(piece):
        for hop in range(1, hops + 1):
            for to_right in (True, False):
                x_copy(hop, piece, to_right).wait_send()

    def exchange(source, landing, send, recv):
        return [
            pltpu.make_async_remote_copy(
                src_ref=source(lax.rem(mine + step, ndp)),
                dst_ref=landing.at[mine],
                send_sem=send.at[step],
                recv_sem=recv.at[step],
                device_id={"dp": lax.rem(mine + step, ndp)},
                device_id_type=MESH,
            )
            for step in range(1, ndp)
        ]

    lane_group = lax.rem(lax.broadcasted_iota(jnp.int32, (GW, 2 * width), 1), width) // GW
    diagonal = jnp.zeros((GW, 2 * width), jnp.float32)
    for g in range(width // GW):
        diagonal = jnp.where(lane_group == g, stats_ref[g * GW : (g + 1) * GW, :], diagonal)
    packed_stats[:GW, :] = diagonal
    packed_stats[GW:, :] = stats_ref[width:, :]
    packed_sums[...] = jnp.zeros_like(packed_sums)
    for slot in range(n):
        packed_sums[pl.ds(lax.rem(me - slot + n, n), 1), :] = patch_sums[slot, :1, :]
    stats_copies = exchange(lambda other: packed_stats, stats_in, stats_send, stats_recv)
    sums_copies = exchange(lambda other: packed_sums, sums_in, sums_send, sums_recv)
    for copy in stats_copies + sums_copies:
        copy.start()
    stats_in[mine] = packed_stats[...]
    sums_in[mine] = packed_sums[...]

    for slot in range(n):
        origin = lax.rem(me - slot + n, n)
        base = pl.multiple_of(origin * depth, 8)
        gathered = None
        for part in range(parts):
            start, size, offset = window_of(part, depth)
            block = totals[slot, part, :, :size].T[offset : offset + depth]
            gathered = block if gathered is None else gathered + block
        products[pl.ds(base, depth), :] = gathered
    product_copies = exchange(
        lambda other: products.at[pl.ds(pl.multiple_of(other * slab, 8), slab)],
        products_in,
        products_send,
        products_recv,
    )
    for copy in product_copies:
        copy.start()
    products_in[mine] = products[pl.ds(pl.multiple_of(mine * slab, 8), slab), :]
    for copy in stats_copies + sums_copies:
        copy.wait()
    stats_out[...] = sum(stats_in[k] for k in range(ndp))
    sums_out[...] = sum(sums_in[k] for k in range(ndp))
    for copy in product_copies:
        copy.wait()
    out_ref[...] = sum(products_in[k] for k in range(ndp))


def handed(piece, chunks):
    return (lax.rem(piece, 2) == 1) & (piece < 2 * (chunks * 6 // 13))


def line_kernel(
    n, ndp, parts, depth, chunk,
    x_hbm, cot_hbm, w_hbm,
    out_ref, stats_out, sums_out,
    stats, packed_stats, stats_in, packed_sums, sums_in, products, products_in,
    held, cot, weights, padded, totals, patch_sums, bank,
    mate_part, mate_stats, whole_sums, mate_products,
    own_send, own_recv, mid_send, mid_recv, pass_send, pass_recv,
    out1_send, out1_recv, out2_send, out2_recv, cot_send, cot_recv,
    w_send, w_recv, local_sem,
    stats_send, stats_recv, sums_send, sums_recv, products_send, products_recv,
    mate_send, mate_recv, last_send, last_recv,
):
    me = lax.axis_index("group")
    mine = lax.axis_index("dp")
    inner = (me == 1) | (me == 2)
    outer = (me == 0) | (me == 3)
    mate = me + 1 - 2 * lax.rem(me, 2)
    across = 3 - me
    beyond = 3 - mate
    rows = x_hbm.shape[0]
    chunks = rows // chunk
    width = w_hbm.shape[1]
    slab = w_hbm.shape[0]

    own_x = pltpu.make_async_copy(x_hbm, held.at[me], local_sem.at[0])
    own_cot = pltpu.make_async_copy(cot_hbm, cot.at[0], local_sem.at[1])
    own_w = pltpu.make_async_copy(w_hbm, weights.at[0, mine], local_sem.at[2])
    own_x.start()
    own_cot.start()
    own_w.start()

    barrier = pltpu.get_barrier_semaphore()
    for step in range(1, ndp):
        pl.semaphore_signal(
            barrier, inc=1, device_id={"dp": lax.rem(mine + step, ndp)}, device_id_type=MESH
        )
    pl.semaphore_signal(barrier, inc=1, device_id={"group": mate}, device_id_type=MESH)

    @pl.when(inner)
    def _():
        pl.semaphore_signal(barrier, inc=1, device_id={"group": across}, device_id_type=MESH)
        pl.semaphore_wait(barrier, ndp + 1)

    @pl.when(outer)
    def _():
        pl.semaphore_wait(barrier, ndp)

    def remote(source, target, send, recv, to):
        return pltpu.make_async_remote_copy(
            src_ref=source, dst_ref=target, send_sem=send, recv_sem=recv,
            device_id=to, device_id_type=MESH,
        )

    def w_copy(step):
        return remote(
            w_hbm, weights.at[0, mine], w_send.at[step], w_recv.at[step],
            {"dp": lax.rem(mine + step, ndp)},
        )

    def span_of(piece):
        return pl.ds(pl.multiple_of(piece * chunk, chunk), chunk)

    to_mate, to_across = {"group": mate}, {"group": across}

    def block(origin, piece, send, recv, to, own=False):
        span = span_of(piece)
        return remote(
            x_hbm.at[span] if own else held.at[origin, span],
            held.at[origin, span], send.at[piece], recv.at[piece], to,
        )

    def own_copy(piece):
        return block(me, piece, own_send, own_recv, to_mate, True)

    def mid_copy(piece):
        return block(me, piece, mid_send, mid_recv, to_across, True)

    def pass_copy(piece):
        return block(mate, piece, pass_send, pass_recv, to_across)

    def out1_copy(piece):
        return block(across, piece, out1_send, out1_recv, to_mate)

    def out2_copy(piece):
        return block(beyond, piece, out2_send, out2_recv, to_mate)

    def cot_copy(piece):
        span = span_of(piece)
        return remote(
            cot_hbm.at[:, span], cot.at[1, :, span], cot_send.at[piece], cot_recv.at[piece],
            to_mate,
        )

    mate_w = remote(weights.at[0], weights.at[1], mate_send.at[0], mate_recv.at[0], to_mate)
    mate_p = remote(mate_part, mate_products, last_send.at[0], last_recv.at[0], to_mate)
    mate_s = remote(packed_stats.at[1], mate_stats, mate_send.at[1], mate_recv.at[1], to_mate)
    mate_x = remote(whole_sums, sums_out, last_send.at[1], last_recv.at[1], to_mate)

    for step in range(1, ndp):
        w_copy(step).start()

    @pl.when(inner)
    def _():
        for piece in range(min(LEAD, chunks)):
            mid_copy(piece).start()

    @pl.when(outer)
    def _():
        for piece in range(min(LEAD, chunks)):
            own_copy(piece).start()

    totals[...] = jnp.zeros_like(totals)
    patch_sums[...] = jnp.zeros_like(patch_sums)
    stats[...] = jnp.zeros_like(stats)
    padded[...] = jnp.zeros_like(padded)
    own_w.wait()
    for step in range(1, ndp):
        w_copy(step).wait()
    per = depth // slab

    def pad_weights(which):
        for j in range(n):
            for part in range(parts):
                offset = window_of(part, depth)[2]
                for k in range(per):
                    padded[which, j, part, offset + k * slab : offset + (k + 1) * slab, :] = (
                        weights[which, j * per + k]
                    )

    @pl.when(outer)
    def _():
        mate_w.start()

        @pl.loop(0, chunks)
        def _(piece):
            @pl.when(piece >= LEAD)
            def _():
                own_copy(piece).start()

            @pl.when(handed(piece, chunks))
            def _():
                cot_copy(piece).start()

    pad_weights(0)
    own_x.wait()
    own_cot.wait()
    ones = jnp.ones((16, chunk), jnp.bfloat16)

    def compute(piece, which):
        span = span_of(piece)
        for part in range(parts):
            start, size, _ = window_of(part, depth)
            embedded = jnp.zeros((chunk, width), jnp.float32)
            for slot in range(n):
                embedded += jnp.dot(
                    held[slot, span, start : start + size],
                    padded[which, slot, part, :size, :],
                    preferred_element_type=jnp.float32,
                )
            bank[:, :width] = embedded.astype(jnp.bfloat16)
            bank[:, width:] = cot[which, part, span, :]
            both = bank[...]
            flipped = both.T
            stats[which, :width, :] += jnp.dot(
                flipped[:width], both, preferred_element_type=jnp.float32
            )
            stats[which, width:, :] += jnp.dot(ones, both, preferred_element_type=jnp.float32)[:8]
            for slot in range(n):
                totals[which, slot, part, :, :size] += jnp.dot(
                    flipped,
                    held[slot, span, start : start + size],
                    preferred_element_type=jnp.float32,
                )

    def add_sums(piece):
        for slot in range(n):
            patch_sums[slot] += jnp.dot(
                ones, held[slot, span_of(piece), :], preferred_element_type=jnp.float32
            )[:8]

    def exchange(source, landing, send, recv):
        return [
            remote(
                source(lax.rem(mine + step, ndp)), landing.at[mine],
                send.at[step], recv.at[step], {"dp": lax.rem(mine + step, ndp)},
            )
            for step in range(1, ndp)
        ]

    def product_copies(which):
        return exchange(
            lambda other: products.at[which, pl.ds(pl.multiple_of(other * slab, 8), slab)],
            products_in.at[which], products_send.at[which], products_recv.at[which],
        )

    lane_group = lax.rem(lax.broadcasted_iota(jnp.int32, (GW, 2 * width), 1), width) // GW

    def pack_stats(which):
        diagonal = jnp.zeros((GW, 2 * width), jnp.float32)
        for g in range(width // GW):
            diagonal = jnp.where(
                lane_group == g, stats[which, g * GW : (g + 1) * GW, :], diagonal
            )
        packed_stats[which, :GW, :] = diagonal
        packed_stats[which, GW:, :] = stats[which, width:, :]

    def send_products(which):
        for slot in range(n):
            gathered = None
            for part in range(parts):
                start, size, offset = window_of(part, depth)
                rows_here = totals[which, slot, part, :, :size].T[offset : offset + depth]
                gathered = rows_here if gathered is None else gathered + rows_here
            products[which, slot * depth : (slot + 1) * depth, :] = gathered
        for copy in product_copies(which):
            copy.start()
        products_in[which, mine] = products[
            which, pl.ds(pl.multiple_of(mine * slab, 8), slab), :
        ]

    given = 2 * (chunks * 6 // 13)

    @pl.when(inner)
    def _():
        @pl.loop(0, chunks + LEAD)
        def _(step):
            @pl.when(step + LEAD < chunks)
            def _():
                mid_copy(step + LEAD).start()

            @pl.when(step < chunks)
            def _():
                own_copy(step).wait_recv()
                pass_copy(step).start()
                mid_copy(step).wait_recv()

                @pl.when(jnp.logical_not(handed(step, chunks)))
                def _():
                    own_copy(step).start()
                    out1_copy(step).start()

            @pl.when(step == LEAD)
            def _():
                mate_w.wait_recv()
                pad_weights(1)

            piece = step - LEAD

            @pl.when(piece >= 0)
            def _():
                pass_copy(piece).wait_recv()

                @pl.when(jnp.logical_not(handed(piece, chunks)))
                def _():
                    out2_copy(piece).start()

                compute(piece, 0)
                add_sums(piece)

                @pl.when(handed(piece, chunks))
                def _():
                    cot_copy(piece).wait_recv()
                    compute(piece, 1)

            @pl.when(piece == given)
            def _():
                pack_stats(1)
                mate_s.start()
                send_products(1)

    @pl.when(outer)
    def _():
        @pl.loop(0, chunks)
        def _(piece):
            @pl.when(jnp.logical_not(handed(piece, chunks)))
            def _():
                own_copy(piece).wait_recv()
                out1_copy(piece).wait_recv()
                out2_copy(piece).wait_recv()
                compute(piece, 0)

        mate_s.wait_recv()

    pack_stats(0)

    @pl.when(outer)
    def _():
        packed_stats[0] = packed_stats[0] + mate_stats[...]

    packed_sums[...] = jnp.zeros_like(packed_sums)
    for slot in range(n):
        packed_sums[slot : slot + 1, :] = patch_sums[slot, :1, :]
    stats_copies = exchange(lambda other: packed_stats.at[0], stats_in, stats_send, stats_recv)
    sums_copies = exchange(lambda other: packed_sums, sums_in, sums_send, sums_recv)
    for copy in sums_copies + stats_copies:
        copy.start()
    stats_in[mine] = packed_stats[0]
    sums_in[mine] = packed_sums[...]
    send_products(0)

    @pl.when(inner)
    def _():
        for copy in product_copies(1):
            copy.wait()
        mate_part[...] = sum(products_in[1, k] for k in range(ndp))
        mate_p.start()

    for copy in sums_copies:
        copy.wait()
    whole_sums[...] = sum(sums_in[k] for k in range(ndp))

    @pl.when(inner)
    def _():
        mate_x.start()
        sums_out[...] = whole_sums[...]

    for copy in stats_copies:
        copy.wait()
    stats_out[...] = sum(stats_in[k] for k in range(ndp))

    @pl.loop(0, chunks)
    def _(piece):
        @pl.when(inner)
        def _():
            mid_copy(piece).wait_send()
            pass_copy(piece).wait_send()

            @pl.when(jnp.logical_not(handed(piece, chunks)))
            def _():
                own_copy(piece).wait_send()
                out1_copy(piece).wait_send()
                out2_copy(piece).wait_send()

        @pl.when(outer)
        def _():
            own_copy(piece).wait_send()

            @pl.when(handed(piece, chunks))
            def _():
                cot_copy(piece).wait_send()

    for copy in product_copies(0):
        copy.wait()
    out_ref[...] = sum(products_in[0, k] for k in range(ndp))

    @pl.when(inner)
    def _():
        mate_s.wait_send()
        mate_p.wait_send()
        mate_x.wait_send()

    @pl.when(outer)
    def _():
        mate_w.wait_send()
        mate_x.wait_recv()
        mate_p.wait_recv()
        out_ref[...] = out_ref[...] + mate_products[...]


def line_products(packed, cotangent, embed_weight, parts, depth, chunk, stats_shape, sums_shape):
    n, ndp = lax.axis_size("group"), lax.axis_size("dp")
    rows, lanes = packed.shape
    slab, width = embed_weight.shape
    chunks = rows // chunk
    window = max(window_of(q, depth)[1] for q in range(parts))
    anywhere = pl.BlockSpec(memory_space=pl.ANY)
    in_vmem = pl.BlockSpec(memory_space=pltpu.VMEM)
    pieces = pltpu.SemaphoreType.DMA((chunks,))
    peers = pltpu.SemaphoreType.DMA((ndp,))
    pair = pltpu.SemaphoreType.DMA((2,))
    both_peers = pltpu.SemaphoreType.DMA((2, ndp))
    return pl.pallas_call(
        functools.partial(line_kernel, n, ndp, parts, depth, chunk),
        out_shape=(
            jax.ShapeDtypeStruct((slab, 2 * width), jnp.float32),
            jax.ShapeDtypeStruct(stats_shape, jnp.float32),
            jax.ShapeDtypeStruct(sums_shape, jnp.float32),
        ),
        in_specs=[anywhere] * 3,
        out_specs=(in_vmem,) * 3,
        scratch_shapes=[
            pltpu.VMEM((2, width + 8, 2 * width), jnp.float32),
            pltpu.VMEM((2,) + stats_shape, jnp.float32),
            pltpu.VMEM((ndp,) + stats_shape, jnp.float32),
            pltpu.VMEM(sums_shape, jnp.float32),
            pltpu.VMEM((ndp,) + sums_shape, jnp.float32),
            pltpu.VMEM((2, n * depth, 2 * width), jnp.float32),
            pltpu.VMEM((2, ndp, slab, 2 * width), jnp.float32),
            pltpu.VMEM((n, rows, lanes), jnp.bfloat16),
            pltpu.VMEM((2, parts, rows, width), jnp.bfloat16),
            pltpu.VMEM((2, ndp, slab, width), jnp.bfloat16),
            pltpu.VMEM((2, n, parts, window, width), jnp.bfloat16),
            pltpu.VMEM((2, n, parts, 2 * width, window), jnp.float32),
            pltpu.VMEM((n, 8, lanes), jnp.float32),
            pltpu.VMEM((chunk, 2 * width), jnp.bfloat16),
            pltpu.VMEM((slab, 2 * width), jnp.float32),
            pltpu.VMEM(stats_shape, jnp.float32),
            pltpu.VMEM(sums_shape, jnp.float32),
            pltpu.VMEM((slab, 2 * width), jnp.float32),
            *[pieces] * 12,
            peers, peers,
            pltpu.SemaphoreType.DMA((3,)),
            peers, peers, peers, peers, both_peers, both_peers,
            pair, pair, pair, pair,
        ],
        compiler_params=pltpu.CompilerParams(
            collective_id=1, has_side_effects=True, vmem_limit_bytes=60 << 20
        ),
    )(packed, cotangent.reshape(parts, rows, width), embed_weight)


def token_products(patches, embed_weight, cotangent):
    n, ndp = lax.axis_size("group"), lax.axis_size("dp")
    tok_rows, depth = patches.shape
    width = embed_weight.shape[1]
    parts = 128 // math.gcd(depth, 128)
    rows = tok_rows // parts
    packed = jnp.concatenate(
        [patches[q * rows : (q + 1) * rows] for q in range(parts)], axis=1
    )
    chunk = 256
    while rows % chunk:
        chunk //= 2
    chunks = rows // chunk
    hops = n // 2
    lanes = parts * depth
    window = max(window_of(q, depth)[1] for q in range(parts))
    anywhere = pl.BlockSpec(memory_space=pl.ANY)
    in_vmem = pl.BlockSpec(memory_space=pltpu.VMEM)
    slab = embed_weight.shape[0]
    stats_shape = (GW + 8, 2 * width)
    sums_shape = (-(-n // 8) * 8, lanes)
    peers = pltpu.SemaphoreType.DMA((ndp,))
    if n == 4 and 3 <= chunks:
        return line_products(
            packed, cotangent, embed_weight, parts, depth, chunk, stats_shape, sums_shape
        )
    ring = pltpu.SemaphoreType.DMA((hops, chunks))
    return pl.pallas_call(
        functools.partial(token_kernel, n, ndp, parts, depth, chunk),
        out_shape=(
            jax.ShapeDtypeStruct((slab, 2 * width), jnp.float32),
            jax.ShapeDtypeStruct(stats_shape, jnp.float32),
            jax.ShapeDtypeStruct(sums_shape, jnp.float32),
        ),
        in_specs=[anywhere] * 3,
        out_specs=(in_vmem,) * 3,
        scratch_shapes=[
            pltpu.VMEM((width + 8, 2 * width), jnp.float32),
            pltpu.VMEM(stats_shape, jnp.float32),
            pltpu.VMEM((ndp,) + stats_shape, jnp.float32),
            pltpu.VMEM(sums_shape, jnp.float32),
            pltpu.VMEM((ndp,) + sums_shape, jnp.float32),
            pltpu.VMEM((n * depth, 2 * width), jnp.float32),
            pltpu.VMEM((ndp, slab, 2 * width), jnp.float32),
            pltpu.VMEM((n, rows, lanes), jnp.bfloat16),
            pltpu.VMEM((tok_rows, width), jnp.bfloat16),
            pltpu.VMEM((ndp,) + embed_weight.shape, jnp.bfloat16),
            pltpu.VMEM((n, parts, window, width), jnp.bfloat16),
            pltpu.VMEM((n, parts, 2 * width, window), jnp.float32),
            pltpu.VMEM((n, 8, lanes), jnp.float32),
            pltpu.VMEM((chunk, 2 * width), jnp.bfloat16),
            ring, ring, ring, ring,
            peers, peers,
            pltpu.SemaphoreType.DMA((3,)),
            peers, peers, peers, peers, peers, peers,
        ],
        compiler_params=pltpu.CompilerParams(
            collective_id=0, has_side_effects=True, vmem_limit_bytes=60 << 20
        ),
    )(packed, cotangent, embed_weight)


def body(patches, embed_weight, channel_gain, cotangent):
    tok_rows = patches.shape[0]
    total_tokens = tok_rows * lax.axis_size("dp")
    loss_scale = 1.0 / math.sqrt(total_tokens)
    identity = jnp.eye(GW, dtype=jnp.float32)
    width_here = embed_weight.shape[1]
    gain_here = lax.dynamic_slice_in_dim(
        channel_gain, lax.axis_index("group") * width_here, width_here
    )
    patch_products, stats, packed_sums = token_products(patches, embed_weight, cotangent)
    n, depth, slab = lax.axis_size("group"), patches.shape[1], embed_weight.shape[0]
    raw_products = stats[:GW, :width_here].reshape(GW, -1, GW).transpose(1, 0, 2)
    cross = stats[:GW, width_here:].reshape(GW, -1, GW).transpose(1, 2, 0)
    sums = stats[GW]
    patch_sums = jnp.sum(packed_sums[:n].reshape(n, -1, depth), axis=1).reshape(-1)
    patch_sums = lax.dynamic_slice_in_dim(patch_sums, lax.axis_index("dp") * slab, slab)[:, None]
    return finish(
        raw_products, cross, sums, patch_products, patch_sums,
        gain_here, loss_scale, total_tokens, identity,
    )


def finish(
    raw_products, cross, sums, patch_products, patch_sums,
    gain_here, loss_scale, total_tokens, identity,
):
    width_here = gain_here.shape[0]
    mean_groups = (sums[:width_here] / total_tokens).reshape(-1, GW)
    cot_sums = sums[width_here:].reshape(-1, GW)
    covariance = (
        raw_products / total_tokens
        - jnp.einsum("ga,gb->gab", mean_groups, mean_groups, precision=highest)
        + EPSILON * identity
    )
    whitener, pullback = jax.vjp(whiten_matrix, covariance)
    cross = loss_scale * (
        cross - jnp.einsum("ga,gb->gab", cot_sums, mean_groups, precision=highest)
    )
    gain_grad = jnp.sum(cross * whitener, axis=2).reshape(-1)
    scale = loss_scale * gain_here
    (grad_cov,) = pullback(cross * gain_here.reshape(-1, GW)[:, :, None])
    symmetric = (grad_cov + jnp.swapaxes(grad_cov, 1, 2)) / total_tokens
    rows = patch_products.shape[0]
    feat_part = patch_products[:, :width_here] - patch_sums * mean_groups.reshape(-1)
    cot_part = scale * (
        patch_products[:, width_here : 2 * width_here]
        - patch_sums * (cot_sums.reshape(-1) / total_tokens)
    )
    weight_grad = jnp.einsum(
        "rga,gab->rgb", cot_part.reshape(rows, -1, GW), whitener, precision=highest
    ) + jnp.einsum("rgb,gcb->rgc", feat_part.reshape(rows, -1, GW), symmetric, precision=highest)
    return (weight_grad.reshape(rows, -1), gain_grad)


def solution(mesh):
    placed = (P("dp", "group"), P("dp", "group"), P(), P("dp", "group"))
    return jax.shard_map(
        body, mesh=mesh, in_specs=placed, out_specs=(P("dp", "group"), P("group")), check_vma=False
    )
```
